256 devices in a mesh: group: 16 (over x_lo, z), shard: 16 (over x_hi, y, core).
Axes of the slice: x: 4 (x_hi: 2, x_lo: 2; x = x_hi * 2 + x_lo), y: 4, z: 8, core: 2. Of those that a mesh axis runs over, the one named last changes fastest.
Arguments:
- queries: bfloat16 [2, 3, 32768, 512], P(None, None, ('group', 'shard')), may hold values from -6 to 6
- key_tokens: bfloat16 [2, 3, 32768, 512], P(None, None, ('group', 'shard')), may hold values from -24 to 24
- value_tokens: bfloat16 [2, 3, 32768, 512], P(None, None, ('group', 'shard')), may hold values from -24 to 24
- token_rate: float32 [2, 3, 32768], P(None, None, ('group', 'shard')), may hold values from 0.1 to 1
- state_in: float32 [16, 3, 512, 3, 512], P('group', None, 'shard'), may hold values from -0.25 to 0.25
- init_state: float32 [3, 512, 3, 512], P(None, 'shard'), may hold values from -0.25 to 0.25
- norm_gain: float32 [3, 512], replicated, may hold values from 0.25 to 2.5
Outputs:
- head_output: bfloat16 [2, 3, 32768, 512], P(None, None, ('group', 'shard'))
- state_out: float32 [16, 3, 512, 3, 512], P('group', None, 'shard')
The draws below stay inside these ranges and needn't reach their ends.
All inputs are finite; a program needn't handle non-finite values.
Results may differ from the reference program's by a relative error of at most 0.011.
Values may be sent and summed in bfloat16 or wider, within the bound.
A program may use at most 128 MiB of HBM per device.

```python
import math
import jax
import jax.numpy as jnp
from jax import lax

D = 512
FH = 512
HEADS = 3
TOK_DEV = 128
SECTIONS = 16
TOKENS = 32768
N_GROUP = 16
N_SHARD = 16


def raised(drawn, rng, source, target, shards_of, factor):
    def block_of(axis_at):
        return (jnp.arange(drawn.shape[axis_at]) // (drawn.shape[axis_at] // shards_of)).reshape((-1,) + (1,) * (drawn.ndim - 1 - axis_at))

    near = jax.random.permutation(rng, shards_of)[block_of(target)]
    second = (block_of(target) + shards_of // 2) % shards_of
    return jnp.where((block_of(source) == near) | (block_of(source) == second), factor * drawn, drawn)


def steps_of(own_key, dims, shards, least, high):
    loudness, own = 1.0, jax.random.fold_in(own_key, 6)
    for axis_at, parts in shards:
        steps = jnp.exp(jax.random.uniform(jax.random.fold_in(own, axis_at), (parts,), jnp.float32, least / len(shards), high / len(shards)))
        loudness = loudness * jnp.repeat(steps, dims[axis_at] // parts).reshape([-1 if axis == axis_at else 1 for axis in range(len(dims))])
    return loudness


def normal_values(key, shape, spread, bound, split=(), kind=jnp.bfloat16):
    array = jax.random.normal(key, shape, jnp.float32) * spread
    if len(split) > 0:
        array = steps_of(key, shape, split, -0.22, 0.18) * array
    return jnp.clip(array, min=-bound, max=bound).astype(kind)


def noise_with(stream_key, shape, spread, bound, split, heavy, held_as=jnp.bfloat16):
    result = spread * jax.random.normal(stream_key, shape, jnp.float32)
    if split:
        result = result * steps_of(stream_key, shape, split, -0.22, 0.18)
    return jnp.clip(raised(result, jax.random.fold_in(stream_key, 3), *heavy), -bound, bound).astype(held_as)


def setup_inputs(seed: int = 0) -> dict:
    key_list = jax.random.split(jax.random.key(seed), 8)
    return {
        "queries": normal_values(key_list[0], (2, HEADS, TOKENS, D), 1.0, 6.0, ((2, 256),)),
        "key_tokens": noise_with(key_list[1], (2, HEADS, TOKENS, D), 1.0, 24.0, ((2, 256),), (2, 3, 256, 6.0)),
        "value_tokens": noise_with(key_list[2], (2, HEADS, TOKENS, D), 1.0, 24.0, ((2, 256),), (2, 3, 256, 6.0)),
        "token_rate": jnp.clip(jnp.exp(math.log(1.0) - 2.3025851 * jax.random.uniform(key_list[3], (2, HEADS, TOKENS), jnp.float32) ** steps_of(key_list[3], (2, HEADS, TOKENS), ((2, 256),), -0.2, 0.2)), 0.1, 1.0),
        "state_in": normal_values(key_list[4], (SECTIONS, HEADS, D, 3, FH), D ** -0.5, 0.25, ((0, 16), (2, 16)), jnp.float32),
        "init_state": normal_values(key_list[5], (HEADS, D, 3, FH), D ** -0.5, 0.25, ((1, 16),), jnp.float32),
        "norm_gain": jnp.clip(jnp.exp(jax.random.uniform(key_list[6], (HEADS, D), jnp.float32, math.log(0.25), math.log(2.5))), 0.25, 2.5),
    }


epsilon = 1e-06

def forward(rows, packed):
    pre_gate = jnp.dot(rows, packed[:, 0], preferred_element_type=jnp.float32)
    pre_up = jnp.dot(rows, packed[:, 1], preferred_element_type=jnp.float32)
    sigmoid_gate = jax.nn.sigmoid(pre_gate)
    hidden = (pre_gate * sigmoid_gate * pre_up).astype(jnp.bfloat16)
    produced = lax.dot_general(hidden, packed[:, 2], (((1,), (1,)), ((), ())), preferred_element_type=jnp.float32)
    return (pre_gate, pre_up, sigmoid_gate, hidden, produced)

def section_head(weights, query_rows, key_rows, value_rows, rate_row, gain_row):
    packed = weights.astype(jnp.bfloat16)
    applied = forward(query_rows, packed)[4]
    normed = applied * lax.rsqrt(lax.optimization_barrier(jnp.mean(applied * applied, axis=-1, keepdims=True)) + epsilon) * gain_row
    pre_gate, pre_up, sigmoid_gate, hidden, guess = forward(key_rows, packed)
    error = (rate_row[:, None] * (guess - value_rows.astype(jnp.float32))).astype(jnp.bfloat16)
    back_hidden = jnp.dot(error, packed[:, 2], preferred_element_type=jnp.float32)
    grad_gate = (back_hidden * pre_up * sigmoid_gate * (1.0 + pre_gate * (1.0 - sigmoid_gate))).astype(jnp.bfloat16)
    grad_up = (back_hidden * pre_gate * sigmoid_gate).astype(jnp.bfloat16)
    contract = (((0,), (0,)), ((), ()))
    gate_part = lax.dot_general(key_rows, grad_gate, contract, preferred_element_type=jnp.float32)
    up_part = lax.dot_general(key_rows, grad_up, contract, preferred_element_type=jnp.float32)
    down_part = lax.dot_general(error, hidden, contract, preferred_element_type=jnp.float32)
    summed = jnp.stack([gate_part, up_part, down_part], axis=1)
    updated = weights - summed / float(TOK_DEV * N_SHARD)
    return (normed.astype(jnp.bfloat16), updated)

def reference(queries, key_tokens, value_tokens, token_rate, state_in, init_state, norm_gain):
    span = TOK_DEV * N_SHARD

    def slot_pass(slot_index, weights_all):

        def per_section(section_index):
            begin = (section_index * span).astype(jnp.int32)

            def per_head(head_index):
                query_rows = lax.dynamic_slice_in_dim(queries[slot_index][head_index], begin, span, 0)
                key_rows = lax.dynamic_slice_in_dim(key_tokens[slot_index][head_index], begin, span, 0)
                value_rows = lax.dynamic_slice_in_dim(value_tokens[slot_index][head_index], begin, span, 0)
                rate_row = lax.dynamic_slice_in_dim(token_rate[slot_index][head_index], begin, span, 0)
                return section_head(weights_all[section_index][head_index], query_rows, key_rows, value_rows, rate_row, norm_gain[head_index])
            return lax.map(per_head, jnp.arange(HEADS, dtype=jnp.int32))
        outputs, updated = lax.map(per_section, jnp.arange(N_GROUP, dtype=jnp.int32))
        outputs = jnp.transpose(outputs, (1, 0, 2, 3)).reshape(HEADS, TOKENS, D)
        return (outputs, updated)
    first_out, middle = slot_pass(0, state_in)
    arrived = jnp.concatenate([init_state[None], middle[:-1]], axis=0)
    second_out, final = slot_pass(1, arrived)
    return (jnp.stack([first_out, second_out], axis=0), final)
```

```python
import functools

import jax
import jax.numpy as jnp
from jax import lax
from jax.experimental import pallas as pl
from jax.experimental.pallas import tpu as pltpu
from jax.sharding import PartitionSpec as P

MESH = pl.DeviceIdType.MESH
epsilon = 1e-06
f32, bf16 = jnp.float32, jnp.bfloat16

GAP = 5
LAG = {
    "issue": -1, "own": 1, "pair": 0, "across": 1, "gathered": 2, "compute": 2,
    "chip": 3, "ring1": 4, "ring2": 4, "update": 6,
}
ORDER = ("ring1", "update", "issue", "gathered", "own", "across", "pair", "chip", "compute", "ring2")
COPIES = 27


def kernel(
    heads, groups,
    q_hbm, k_hbm, v_hbm, rate_hbm, state_hbm, init_hbm, gain_ref,
    out_ref, state_out_ref,
    q, k, v, rate, init, cur, w, grad, acc, fin, last, moved, land_c, land_y, land_x, land_s,
    in_sem, send_sem, recv_sem,
):
    g = lax.axis_index("group")
    me = lax.axis_index("shard")
    x, y, c = me // 8, (me // 2) % 4, me % 2
    xo, co = 1 - x, 1 - c
    yp, ym, yo = (y + 1) % 4, (y + 3) % 4, (y + 2) % 4
    up, down = (g, x * 8 + yp * 2 + c), (g, x * 8 + ym * 2 + c)
    pair, sib = (g, xo * 8 + y * 2 + c), (g, x * 8 + y * 2 + co)
    ahead, behind = ((g + 1) % groups, me), ((g + groups - 1) % groups, me)
    jobs = 2 * heads
    rows = w.shape[5]
    half = rows // 2
    A, B, ALL = pl.ds(0, half), pl.ds(half, half), pl.ds(0, rows)

    def W(j, px, py, pc, part=ALL):
        return w.at[j, :, px, py, pc, part, :]

    def C(j, py, part=ALL):
        return acc.at[j, :, :, py, part, :]

    def table(n, j):
        if n < 16:
            sent = {
                0: (W(j, x, y, c), up, W(j, x, ym, c)),
                1: (W(j, x, y, c), down, W(j, x, yp, c)),
                2: (W(j, x, y, c), pair, W(j, xo, y, c)),
                3: (W(j, x, y, c), sib, W(j, x, y, co)),
                4: (W(j, xo, y, c), up, W(j, xo, ym, c)),
                5: (W(j, xo, y, c), down, W(j, xo, yp, c)),
                6: (W(j, xo, y, c), sib, W(j, xo, y, co)),
                7: (W(j, x, ym, c, A), up, W(j, x, yo, c, A)),
                8: (W(j, x, yp, c, B), down, W(j, x, yo, c, B)),
                9: (W(j, x, ym, c), sib, W(j, x, ym, co)),
                10: (W(j, x, yp, c), sib, W(j, x, yp, co)),
                11: (W(j, xo, ym, c, A), up, W(j, xo, yo, c, A)),
                12: (W(j, xo, yp, c, B), down, W(j, xo, yo, c, B)),
                13: (W(j, xo, ym, c), sib, W(j, xo, ym, co)),
                14: (W(j, xo, yp, c), sib, W(j, xo, yp, co)),
                15: (w.at[j, :, :, yo, c], sib, w.at[j, :, :, yo, co]),
            }[n]
            return sent[0], sent[0], sent[1], sent[2]
        if n < 19:
            m = n - 16
            return grad.at[j, m, :, :, co], land_c.at[j, m], sib, land_c.at[j, m]
        if n < 25:
            src, to = {
                19: (C(j, yo, A), up), 20: (C(j, yo, B), down),
                21: (C(j, yp, B), up), 22: (C(j, ym, A), down),
                23: (C(j, yp, A), up), 24: (C(j, ym, B), down),
            }[n]
            return src, land_y.at[j, n - 19], to, land_y.at[j, n - 19]
        if n == 25:
            return last.at[j], land_x.at[j], pair, land_x.at[j]
        return moved.at[j], land_s.at[j], ahead, land_s.at[j]

    def copy(n, j):
        src, dst, to, here = table(n, j)
        return pltpu.make_async_remote_copy(
            src_ref=src, dst_ref=dst, send_sem=send_sem.at[j, n], recv_sem=recv_sem.at[j, n],
            device_id=to, device_id_type=MESH,
        )

    def send(j, *which):
        for n in which:
            copy(n, j).start()

    def arrived(j, *which):
        for n in which:
            src, dst, to, here = table(n, j)
            pltpu.make_async_remote_copy(
                src_ref=here, dst_ref=here, send_sem=send_sem.at[j, n], recv_sem=recv_sem.at[j, n],
                device_id=to, device_id_type=MESH,
            ).wait_recv()

    def issue(j):
        arrived(j - heads, 26)
        start = jnp.where(g == 0, init[j - heads], land_s[j - heads].astype(f32))
        cur[j] = start
        w[j, :, x, y, c] = start.astype(bf16)
        send(j, 0, 1, 2, 3)

    def own(j):
        arrived(j, 0, 1)
        send(j, 7, 8, 9, 10)

    def from_pair(j):
        arrived(j, 2)
        send(j, 4, 5, 6)

    def across(j):
        arrived(j, 4, 5)
        send(j, 11, 12, 13, 14)

    def gathered(j):
        arrived(j, 7, 8, 11, 12)
        send(j, 15)

    def compute(j):
        arrived(j, 3, 6, 9, 10, 13, 14, 15)
        tokens, depth = q.shape[1], q.shape[2]

        def weight(m):
            return w[j, m].reshape(depth, w.shape[6])

        both = jnp.concatenate([q[j], k[j]], axis=0)
        gate = jnp.dot(both, weight(0), preferred_element_type=f32)
        value = jnp.dot(both, weight(1), preferred_element_type=f32)
        sig = jax.nn.sigmoid(gate)
        hidden = (gate * sig * value).astype(bf16)
        made = lax.dot_general(hidden, weight(2), (((1,), (1,)), ((), ())), preferred_element_type=f32)
        applied, guess = made[:tokens], made[tokens:]
        scale = jnp.broadcast_to(rate[j], (depth, tokens)).T
        error = (scale * (guess - v[j].astype(f32))).astype(bf16)
        back = jnp.dot(error, weight(2), preferred_element_type=f32)
        pg, pu, ps = gate[tokens:], value[tokens:], sig[tokens:]
        d_gate = (back * pu * ps * (1.0 + pg * (1.0 - ps))).astype(bf16)
        d_up = (back * pg * ps).astype(bf16)
        key_t, err_t = k[j].T, error.T
        for m, (left, right) in enumerate(((key_t, d_gate), (key_t, d_up), (err_t, hidden[tokens:]))):
            part = jnp.dot(left, right, preferred_element_type=f32)
            grad[j, m] = part.astype(bf16).reshape(grad.shape[2:])
            send(j, 16 + m)
        mean = jnp.mean(applied * applied, axis=-1, keepdims=True)
        normed = applied * lax.rsqrt(mean + epsilon) * gain_ref[lax.rem(j, heads)]
        out_ref[j] = normed.astype(bf16)

    def chip(j):
        for m in range(3):
            arrived(j, 16 + m)
            acc[j, m] = (grad[j, m, :, :, c].astype(f32) + land_c[j, m].astype(f32)).astype(bf16)
        send(j, 19, 20, 21, 22)

    def ring1(j):
        arrived(j, 19)
        acc[j, :, :, yp, A] = (acc[j, :, :, yp, A].astype(f32) + land_y[j, 0].astype(f32)).astype(bf16)
        send(j, 23)
        arrived(j, 20)
        acc[j, :, :, ym, B] = (acc[j, :, :, ym, B].astype(f32) + land_y[j, 1].astype(f32)).astype(bf16)
        send(j, 24)

    def ring2(j):
        arrived(j, 21, 22, 23, 24)

        def total(px):
            first = acc[j, :, px, y, A].astype(f32) + land_y[j, 3, :, px].astype(f32) + land_y[j, 4, :, px].astype(f32)
            second = acc[j, :, px, y, B].astype(f32) + land_y[j, 2, :, px].astype(f32) + land_y[j, 5, :, px].astype(f32)
            return jnp.concatenate([first, second], axis=1)

        last[j] = total(xo).astype(bf16)
        send(j, 25)
        fin[j] = total(x)

    def update(j):
        arrived(j, 25)
        new = cur[j] - (fin[j] + land_x[j].astype(f32)) * (1.0 / float(q.shape[1] * 16))

        @pl.when(j < heads)
        def _():
            moved[j] = new.astype(bf16)
            send(j, 26)

        @pl.when(j >= heads)
        def _():
            state_out_ref[j - heads] = new

    def load(n, src, dst):
        return pltpu.make_async_copy(src, dst, in_sem.at[n])

    loads = [
        load(0, state_hbm, cur.at[pl.ds(0, heads)]), load(1, q_hbm, q), load(2, k_hbm, k), load(3, v_hbm, v),
        load(4, rate_hbm, rate), load(5, init_hbm, init),
    ]
    for one in loads:
        one.start()
    barrier = pltpu.get_barrier_semaphore()
    for other in (up, down, pair, sib, ahead, behind):
        pl.semaphore_signal(barrier, inc=1, device_id=other, device_id_type=MESH)
    loads[0].wait()
    for h in range(heads):
        w[h, :, x, y, c] = cur[h].astype(bf16)
    pl.semaphore_wait(barrier, 6)
    for h in range(heads):
        send(h, 0, 1, 2, 3)
    for one in loads[1:]:
        one.wait()

    stages = {
        "issue": issue, "own": own, "pair": from_pair, "across": across, "gathered": gathered, "compute": compute,
        "chip": chip, "ring1": ring1, "ring2": ring2, "update": update,
    }

    def tick(t, carry):
        for name in ORDER:
            step = t - LAG[name]
            second = step >= heads
            j = jnp.where(second, step - GAP, step)
            good = (step >= 0) & ((step < heads) | ((j >= heads) & (j < jobs)))
            if name == "issue":
                good = good & second

            @pl.when(good)
            def _(name=name, j=j):
                stages[name](j)

        return carry

    lax.fori_loop(0, jobs + GAP + max(LAG.values()), tick, 0)

    def drain(j, carry):
        for n in range(COPIES - 1):
            copy(n, j).wait_send()
        return carry

    lax.fori_loop(0, jobs, drain, 0)
    for h in range(heads):
        copy(26, h).wait_send()


def on_device(queries, key_tokens, value_tokens, token_rate, state_in, init_state, norm_gain):
    slots, heads, tokens, depth = queries.shape
    rows, hidden = init_state.shape[1], init_state.shape[3]
    jobs = slots * heads
    groups = lax.axis_size("group")
    half = rows // 2
    state = jnp.transpose(state_in[0], (0, 2, 1, 3))
    init = jnp.transpose(init_state, (0, 2, 1, 3))
    any_spec, vmem = pl.BlockSpec(memory_space=pl.ANY), pl.BlockSpec(memory_space=pltpu.VMEM)
    V = pltpu.VMEM
    out, new = pl.pallas_call(
        functools.partial(kernel, heads, groups),
        out_shape=(
            jax.ShapeDtypeStruct((jobs, tokens, depth), bf16),
            jax.ShapeDtypeStruct((heads, 3, rows, hidden), f32),
        ),
        in_specs=[any_spec] * 6 + [vmem],
        out_specs=(vmem, vmem),
        scratch_shapes=[
            V((jobs, tokens, depth), bf16), V((jobs, tokens, depth), bf16), V((jobs, tokens, depth), bf16),
            V((jobs, 1, tokens), f32), V((heads, 3, rows, hidden), f32), V((jobs, 3, rows, hidden), f32),
            V((jobs, 3, 2, 4, 2, rows, hidden), bf16), V((jobs, 3, 2, 4, 2, rows, hidden), bf16),
            V((jobs, 3, 2, 4, rows, hidden), bf16), V((jobs, 3, rows, hidden), f32),
            V((jobs, 3, rows, hidden), bf16), V((heads, 3, rows, hidden), bf16),
            V((jobs, 3, 2, 4, rows, hidden), bf16), V((jobs, 6, 3, 2, half, hidden), bf16),
            V((jobs, 3, rows, hidden), bf16), V((heads, 3, rows, hidden), bf16),
            pltpu.SemaphoreType.DMA((6,)), pltpu.SemaphoreType.DMA((jobs, COPIES)),
            pltpu.SemaphoreType.DMA((jobs, COPIES)),
        ],
        compiler_params=pltpu.CompilerParams(
            collective_id=0, has_side_effects=True, vmem_limit_bytes=60 * 1024 * 1024
        ),
    )(
        queries.reshape(jobs, tokens, depth), key_tokens.reshape(jobs, tokens, depth),
        value_tokens.reshape(jobs, tokens, depth), token_rate.reshape(jobs, 1, tokens), state, init,
        norm_gain.reshape(heads, 1, depth),
    )
    return out.reshape(queries.shape), jnp.transpose(new, (0, 2, 1, 3))[None]


def solution(mesh):
    in_specs = (
        P(None, None, ("group", "shard"), None),
        P(None, None, ("group", "shard"), None),
        P(None, None, ("group", "shard"), None),
        P(None, None, ("group", "shard")),
        P("group", None, "shard", None, None),
        P(None, "shard", None, None),
        P(),
    )
    out_specs = (P(None, None, ("group", "shard"), None), P("group", None, "shard", None, None))
    return jax.shard_map(
        on_device, mesh=mesh, in_specs=in_specs, out_specs=out_specs, check_vma=False
    )
```

```python
import functools

import jax
import jax.numpy as jnp
from jax import lax
from jax.experimental import pallas as pl
from jax.experimental.pallas import tpu as pltpu
from jax.sharding import PartitionSpec as P

MESH = pl.DeviceIdType.MESH
epsilon = 1e-06
f32, bf16 = jnp.float32, jnp.bfloat16

SCHEDULE = (
    "issue0", "issue1", "own0", "pair0", "issue2", "own1", "far0", "across0", "pair1", "farpair0", "own2", "far1",
    "compute0", "far2", "pair2", "across1", "farpair1", "chip0", "compute1", "farpair2", "across2", "rfar0",
    "chip1", "compute2", "rcross0", "relay0", "rfar1", "chip2", "update0", "rcross1", "relay1", "rfar2", "issue3",
    "update1", "rcross2", "relay2", "own3", "issue4", "update2", "pair3", "far3", "own4", "issue5", "across3",
    "farpair3", "far4", "pair4", "compute3", "own5", "across4", "farpair4", "pair5", "far5", "compute4", "chip3",
    "across5", "chip4", "farpair5", "compute5", "rcross3", "rfar3", "chip5", "rcross4", "rfar4", "rfar5",
    "rcross5", "relay3", "relay4", "relay5", "update4", "update3", "update5",
)
COPIES = 30


def kernel(
    heads, groups,
    q_hbm, k_hbm, v_hbm, rate_hbm, state_hbm, init_hbm, gain_hbm,
    out_ref, state_out_ref,
    q, k, v, rate, init, gain, cur, w, grad, acc, moved, land_c, land_p, land_x, land_y, land_l, land_s,
    in_sem, send_sem, recv_sem, go_sem,
):
    g = lax.axis_index("group")
    me = lax.axis_index("shard")
    x, y, c = me // 8, (me // 2) % 4, me % 2
    xo, co = 1 - x, 1 - c
    yp, ym, yo = (y + 1) % 4, (y + 3) % 4, (y + 2) % 4
    up, down = (g, x * 8 + yp * 2 + c), (g, x * 8 + ym * 2 + c)
    pair, sib = (g, xo * 8 + y * 2 + c), (g, x * 8 + y * 2 + co)
    ahead, behind = ((g + 1) % groups, me), ((g + groups - 1) % groups, me)
    middle = groups // 2 - 1
    jobs = 2 * heads
    rows = w.shape[5]
    half = rows // 2
    A, B, ALL = pl.ds(0, half), pl.ds(half, half), pl.ds(0, rows)

    def W(j, px, py, pc, part=ALL):
        return w.at[j, :, px, py, pc, part, :]

    def R(j, px, py, part=ALL):
        return acc.at[j, :, px, py, part, :]

    def table(n, j):
        if n < 16:
            sent, to, here = {
                0: (W(j, x, y, c), up, W(j, x, ym, c)),
                1: (W(j, x, y, c), down, W(j, x, yp, c)),
                2: (W(j, x, y, c), pair, W(j, xo, y, c)),
                3: (W(j, x, y, c), sib, W(j, x, y, co)),
                4: (W(j, xo, y, c), up, W(j, xo, ym, c)),
                5: (W(j, xo, y, c), down, W(j, xo, yp, c)),
                6: (W(j, xo, y, c), sib, W(j, xo, y, co)),
                7: (W(j, x, ym, c, A), up, W(j, x, yo, c, A)),
                8: (W(j, x, yp, c, B), down, W(j, x, yo, c, B)),
                9: (W(j, x, ym, c), sib, W(j, x, ym, co)),
                10: (W(j, x, yp, c), sib, W(j, x, yp, co)),
                11: (W(j, x, yo, c), pair, W(j, xo, yo, c)),
                12: (W(j, xo, yo, c), sib, W(j, xo, yo, co)),
                13: (W(j, xo, ym, c), sib, W(j, xo, ym, co)),
                14: (W(j, xo, yp, c), sib, W(j, xo, yp, co)),
                15: (W(j, x, yo, c), sib, W(j, x, yo, co)),
            }[n]
            return sent, sent, to, here
        if n < 19:
            m = n - 16
            return grad.at[j, m, :, :, co], land_c.at[j, m], sib, land_c.at[j, m]
        if n == 19:
            return R(j, xo, yo), land_p.at[j], pair, land_p.at[j]
        if n < 22:
            src, to = ((R(j, xo, yp), up), (R(j, xo, ym), down))[n - 20]
            return src, land_x.at[j, n - 20], to, land_x.at[j, n - 20]
        if n < 28:
            src, to = (
                (R(j, x, yp, B), up), (R(j, x, ym, A), down), (R(j, x, yo, A), up), (R(j, x, yo, B), down),
                (R(j, x, yp, A), up), (R(j, x, ym, B), down),
            )[n - 22]
            return src, land_y.at[j, n - 22], to, land_y.at[j, n - 22]
        if n == 28:
            return R(j, xo, y), land_l.at[j], pair, land_l.at[j]
        return moved.at[j], land_s.at[j], ahead, land_s.at[j]

    def copy(n, j):
        src, dst, to, here = table(n, j)
        return pltpu.make_async_remote_copy(
            src_ref=src, dst_ref=dst, send_sem=send_sem.at[j, n], recv_sem=recv_sem.at[j, n],
            device_id=to, device_id_type=MESH,
        )

    def send(j, *which):
        for n in which:
            copy(n, j).start()

    def arrived(j, *which):
        for n in which:
            src, dst, to, here = table(n, j)
            pltpu.make_async_remote_copy(
                src_ref=here, dst_ref=here, send_sem=send_sem.at[j, n], recv_sem=recv_sem.at[j, n],
                device_id=to, device_id_type=MESH,
            ).wait_recv()

    def issue(j):
        if j >= heads:
            @pl.when(g == 0)
            def _():
                cur[j] = init[j - heads]
                w[j, :, x, y, c] = init[j - heads].astype(bf16)

            @pl.when(g > 0)
            def _():
                arrived(j - heads, 29)
                cur[j] = land_s[j - heads].astype(f32)
                w[j, :, x, y, c] = land_s[j - heads]

        send(j, 0, 1, 2, 3)

    def own(j):
        arrived(j, 0, 1)
        send(j, 7, 8, 9, 10)

    def from_pair(j):
        arrived(j, 2)
        send(j, 4, 5, 6)

    def far(j):
        arrived(j, 7, 8)
        send(j, 11, 15)

    def across(j):
        arrived(j, 4, 5)
        send(j, 13, 14)

    def far_pair(j):
        arrived(j, 11)
        send(j, 12)

    def compute(j):
        arrived(j, 3, 6, 9, 10, 13, 14, 15, 12)
        tokens, depth = q.shape[1], q.shape[2]
        slot, head = divmod(j, heads)

        def weight(m):
            return w[j, m].reshape(depth, w.shape[6])

        both = jnp.concatenate([q[j], k[j]], axis=0)
        gate = jnp.dot(both, weight(0), preferred_element_type=f32)
        value = jnp.dot(both, weight(1), preferred_element_type=f32)
        sig = jax.nn.sigmoid(gate)
        hidden = (gate * sig * value).astype(bf16)
        made = lax.dot_general(hidden, weight(2), (((1,), (1,)), ((), ())), preferred_element_type=f32)
        applied, guess = made[:tokens], made[tokens:]
        scale = jnp.broadcast_to(rate[head, pl.ds(slot, 1)], (depth, tokens)).T
        error = (scale * (guess - v[j].astype(f32))).astype(bf16)
        back = jnp.dot(error, weight(2), preferred_element_type=f32)
        pg, pu, ps = gate[tokens:], value[tokens:], sig[tokens:]
        d_gate = (back * pu * ps * (1.0 + pg * (1.0 - ps))).astype(bf16)
        d_up = (back * pg * ps).astype(bf16)
        key_t, err_t = k[j].T, error.T
        for m, (left, right) in enumerate(((key_t, d_gate), (key_t, d_up), (err_t, hidden[tokens:]))):
            part = jnp.dot(left, right, preferred_element_type=f32)
            grad[j, m] = part.astype(bf16).reshape(grad.shape[2:])
            send(j, 16 + m)
        mean = jnp.mean(applied * applied, axis=-1, keepdims=True)
        normed = applied * lax.rsqrt(mean + epsilon) * gain[pl.ds(head, 1)]
        out_ref[j] = normed.astype(bf16)

    def chip(j):
        for m in range(3):
            arrived(j, 16 + m)
            acc[j, m] = (grad[j, m, :, :, c].astype(f32) + land_c[j, m].astype(f32)).astype(bf16)
        send(j, 20, 21, 19, 22, 23)

    def r_far(j):
        arrived(j, 19)
        acc[j, :, x, yo] = (acc[j, :, x, yo].astype(f32) + land_p[j].astype(f32)).astype(bf16)
        send(j, 24, 25)

    def r_cross(j):
        arrived(j, 20, 21)
        both = land_x[j, 0].astype(f32) + land_x[j, 1].astype(f32)
        acc[j, :, xo, y] = (acc[j, :, xo, y].astype(f32) + both).astype(bf16)
        send(j, 28)

    def relay(j):
        arrived(j, 24)
        acc[j, :, x, yp, A] = (acc[j, :, x, yp, A].astype(f32) + land_y[j, 2].astype(f32)).astype(bf16)
        send(j, 26)
        arrived(j, 25)
        acc[j, :, x, ym, B] = (acc[j, :, x, ym, B].astype(f32) + land_y[j, 3].astype(f32)).astype(bf16)
        send(j, 27)

    def update(j):
        arrived(j, 22, 23, 26, 27, 28)
        first = land_y[j, 1].astype(f32) + land_y[j, 4].astype(f32)
        second = land_y[j, 0].astype(f32) + land_y[j, 5].astype(f32)
        total = acc[j, :, x, y].astype(f32) + jnp.concatenate([first, second], axis=1) + land_l[j].astype(f32)
        new = cur[j] - total * (1.0 / float(q.shape[1] * 16))

        if j >= heads:
            state_out_ref[j - heads] = new
            return

        @pl.when(g < groups - 1)
        def _():
            moved[j] = new.astype(bf16)
            if j == 0:
                @pl.when(g == middle)
                def _():
                    pl.semaphore_wait(go_sem, 1)
            send(j, 29)

    def load(n, src, dst):
        return pltpu.make_async_copy(src, dst, in_sem.at[n])

    loads = [
        load(0, state_hbm, cur.at[pl.ds(0, heads)]), load(1, q_hbm, q), load(2, k_hbm, k), load(3, v_hbm, v),
        load(4, rate_hbm, rate), load(5, init_hbm, init), load(6, gain_hbm, gain),
    ]
    for one in loads:
        one.start()
    barrier = pltpu.get_barrier_semaphore()

    def hello(other):
        pl.semaphore_signal(barrier, inc=1, device_id=other, device_id_type=MESH)

    for other in (up, down, pair, sib):
        hello(other)

    @pl.when((g > 0) & (g != middle + 1))
    def _():
        hello(behind)

    @pl.when((g == middle) | (g == middle + 1))
    def _():
        hello((groups - 1, me))

    loads[0].wait()
    for h in range(heads):
        w[h, :, x, y, c] = cur[h].astype(bf16)
    near = jnp.where(g == middle, 4, jnp.where(g == groups - 1, 6, 5))
    pl.semaphore_wait(barrier, near)

    @pl.when(g == groups - 1)
    def _():
        pl.semaphore_signal(go_sem, inc=1, device_id=(middle, me), device_id_type=MESH)

    stages = {
        "issue": issue, "own": own, "pair": from_pair, "far": far, "across": across, "farpair": far_pair,
        "compute": compute, "chip": chip, "rfar": r_far, "rcross": r_cross, "relay": relay, "update": update,
    }

    waited = False
    for step in SCHEDULE:
        name, j = step[:-1], int(step[-1])
        if name == "compute" and not waited:
            waited = True
            for one in loads[1:]:
                one.wait()
        stages[name](j)

    def drain(j, carry):
        for n in range(COPIES - 1):
            copy(n, j).wait_send()
        return carry

    lax.fori_loop(0, jobs, drain, 0)

    @pl.when(g < groups - 1)
    def _():
        for h in range(heads):
            copy(COPIES - 1, h).wait_send()


def on_device(queries, key_tokens, value_tokens, token_rate, state_in, init_state, norm_gain):
    slots, heads, tokens, depth = queries.shape
    rows, hidden = init_state.shape[1], init_state.shape[3]
    jobs = slots * heads
    groups = lax.axis_size("group")
    half = rows // 2
    state = jnp.transpose(state_in[0], (0, 2, 1, 3))
    init = jnp.transpose(init_state, (0, 2, 1, 3))
    any_spec, vmem = pl.BlockSpec(memory_space=pl.ANY), pl.BlockSpec(memory_space=pltpu.VMEM)
    V = pltpu.VMEM
    out, new = pl.pallas_call(
        functools.partial(kernel, heads, groups),
        out_shape=(
            pltpu.VMEM((jobs, tokens, depth), bf16),
            pltpu.VMEM((heads, 3, rows, hidden), f32),
        ),
        in_specs=[any_spec] * 7,
        out_specs=(vmem, vmem),
        scratch_shapes=[
            V((jobs, tokens, depth), bf16), V((jobs, tokens, depth), bf16), V((jobs, tokens, depth), bf16),
            V((heads, slots, tokens), f32), V((heads, 3, rows, hidden), f32), V((heads, depth), f32),
            V((jobs, 3, rows, hidden), f32),
            V((jobs, 3, 2, 4, 2, rows, hidden), bf16), V((jobs, 3, 2, 4, 2, rows, hidden), bf16),
            V((jobs, 3, 2, 4, rows, hidden), bf16), V((heads, 3, rows, hidden), bf16),
            V((jobs, 3, 2, 4, rows, hidden), bf16), V((jobs, 3, rows, hidden), bf16),
            V((jobs, 2, 3, rows, hidden), bf16), V((jobs, 6, 3, half, hidden), bf16),
            V((jobs, 3, rows, hidden), bf16), V((heads, 3, rows, hidden), bf16),
            pltpu.SemaphoreType.DMA((7,)), pltpu.SemaphoreType.DMA((jobs, COPIES)),
            pltpu.SemaphoreType.DMA((jobs, COPIES)), pltpu.SemaphoreType.REGULAR,
        ],
        compiler_params=pltpu.CompilerParams(
            collective_id=0, has_side_effects=True, vmem_limit_bytes=60 * 1024 * 1024
        ),
    )(
        queries.reshape(jobs, tokens, depth), key_tokens.reshape(jobs, tokens, depth),
        value_tokens.reshape(jobs, tokens, depth), jnp.transpose(token_rate, (1, 0, 2)), state, init,
        norm_gain,
    )
    return out.reshape(queries.shape), jnp.transpose(new, (0, 2, 1, 3))[None]


def solution(mesh):
    in_specs = (
        P(None, None, ("group", "shard"), None),
        P(None, None, ("group", "shard"), None),
        P(None, None, ("group", "shard"), None),
        P(None, None, ("group", "shard")),
        P("group", None, "shard", None, None),
        P(None, "shard", None, None),
        P(),
    )
    out_specs = (P(None, None, ("group", "shard"), None), P("group", None, "shard", None, None))
    return jax.shard_map(
        on_device, mesh=mesh, in_specs=in_specs, out_specs=out_specs, check_vma=False
    )
```

```python
import functools

import jax
import jax.numpy as jnp
from jax import lax
from jax.experimental import pallas as pl
from jax.experimental.pallas import tpu as pltpu
from jax.sharding import PartitionSpec as P

MESH = pl.DeviceIdType.MESH
epsilon = 1e-06
f32, bf16 = jnp.float32, jnp.bfloat16

(
    U0A, U0B, D0A, D0B, X0A, X0B, S0, F7, F8, S9, S10, BU, BD, U4A, U4B, D5A, D5B, S6, GA, GB, S15, S12, S13, S14,
    C0, C1, C2, H19A, H19B, U20A, U20B, D21A, D21B, PA, PB, U22, D23, U24, D25, X28A, X28B, U26, D27, SHIFT_A,
    SHIFT_B, ISA, ISB, KEYS, QUERIES, CHIP, RFA, RFB, RCA, RCB, RLU, RLD, UPA, UPB, R12, R13, R14
) = range(61)
A, B, AB = range(3)
ALL, GATE, REST = range(3)
UP, DOWN, PAIR, SIB = range(4)
SCHEDULE = (
    2, 26, 0, 32, 20, 1, 18, 31, 25, 19, 44, 8, 50, 14, 80, 30, 49, 73, 43, 92, 86, 98, 7, 42, 68, 74, 13, 110,
    116, 38, 79, 62, 48, 104, 122, 97, 24, 37, 109, 103, 96, 56, 115, 134, 67, 91, 36, 121, 140, 66, 85, 128, 84,
    72, 78, 61, 102, 55, 108, 12, 284, 127, 90, 114, 133, 6, 139, 290, 296, 170, 218, 176, 164, 283, 182, 138, 120,
    188, 132, 54, 60, 206, 126, 194, 200, 212, 308, 230, 295, 169, 217, 175, 193, 163, 205, 302, 224, 282, 181,
    211, 320, 242, 332, 254, 314, 236, 307, 229, 187, 326, 248, 294, 162, 199, 186, 301, 223, 174, 168, 192, 319,
    344, 266, 204, 241, 180, 338, 260, 331, 253, 300, 222, 198, 289, 325, 313, 247, 235, 210, 306, 312, 228, 216,
    234, 318, 343, 265, 324, 246, 281, 35, 240, 23, 337, 259, 275, 5, 330, 252, 29, 17, 11, 336, 258, 53, 89, 77,
    47, 71, 101, 342, 264, 280, 34, 22, 83, 274, 28, 41, 16, 4, 95, 119, 10, 113, 273, 40, 3, 52, 59, 65, 137, 27,
    125, 107, 46, 88, 64, 279, 21, 70, 76, 143, 100, 33, 118, 45, 131, 82, 94, 58, 112, 9, 51, 15, 75, 106, 39,
    287, 111, 124, 99, 105, 142, 69, 136, 81, 130, 87, 117, 93, 123, 299, 57, 185, 167, 197, 63, 215, 286, 191,
    203, 293, 135, 173, 129, 141, 323, 179, 245, 305, 227, 221, 298, 190, 166, 285, 178, 220, 202, 209, 311, 184,
    172, 317, 214, 233, 329, 196, 297, 171, 183, 189, 177, 251, 195, 316, 165, 288, 207, 304, 310, 232, 335, 291,
    226, 322, 201, 208, 239, 309, 231, 257, 219, 315, 244, 303, 225, 321, 238, 292, 243, 213, 237, 328, 334, 250,
    256, 333, 255, 327, 249, 341, 340, 347, 346, 345, 339,
)
GATHER = {
    U0A: (0, 0, A, ALL, UP, ()), U0B: (0, 0, B, ALL, UP, ()),
    D0A: (0, 0, A, ALL, DOWN, ()), D0B: (0, 0, B, ALL, DOWN, ()),
    X0A: (0, 0, A, ALL, PAIR, ()), X0B: (0, 0, B, ALL, PAIR, ()),
    S0: (0, 0, AB, ALL, SIB, ()),
    F7: (0, 3, A, ALL, UP, (U0A,)), F8: (0, 1, B, ALL, DOWN, (D0B,)),
    S9: (0, 3, AB, ALL, SIB, (U0A, U0B)), S10: (0, 1, AB, ALL, SIB, (D0A, D0B)),
    BU: (0, 3, A, GATE, PAIR, (U0A,)), BD: (0, 1, B, GATE, PAIR, (D0B,)),
    U4A: (1, 0, A, REST, UP, (X0A,)), U4B: (1, 0, B, ALL, UP, (X0B,)),
    D5A: (1, 0, A, ALL, DOWN, (X0A,)), D5B: (1, 0, B, REST, DOWN, (X0B,)),
    S6: (1, 0, AB, ALL, SIB, (X0A, X0B)),
    GA: (0, 2, A, ALL, PAIR, (F7,)), GB: (0, 2, B, ALL, PAIR, (F8,)),
    S15: (0, 2, AB, ALL, SIB, (F7, F8)), S12: (1, 2, AB, ALL, SIB, (R12,)),
    S13: (1, 3, AB, ALL, SIB, (R13,)), S14: (1, 1, AB, ALL, SIB, (R14,)),
}
REDUCE = {
    H19A: (1, 2, A, ALL, PAIR), H19B: (1, 2, B, ALL, PAIR),
    U20A: (1, 1, A, REST, UP), U20B: (1, 1, B, ALL, UP),
    D21A: (1, 3, A, ALL, DOWN), D21B: (1, 3, B, REST, DOWN),
    PA: (1, 1, A, GATE, PAIR), PB: (1, 3, B, GATE, PAIR),
    U22: (0, 1, B, ALL, UP), D23: (0, 3, A, ALL, DOWN),
    U24: (0, 2, A, ALL, UP), D25: (0, 2, B, ALL, DOWN),
    X28A: (1, 0, A, ALL, PAIR), X28B: (1, 0, B, ALL, PAIR),
    U26: (0, 1, A, ALL, UP), D27: (0, 3, B, ALL, DOWN),
}
ADD = {
    RFA: (0, 2, A, ((H19A, ALL),)), RFB: (0, 2, B, ((H19B, ALL),)),
    RCA: (1, 0, A, ((D21A, ALL), (U20A, REST))), RCB: (1, 0, B, ((U20B, ALL), (D21B, REST))),
    RLU: (0, 1, A, ((U24, ALL), (PA, GATE))), RLD: (0, 3, B, ((D25, ALL), (PB, GATE))),
}
FINAL = {UPA: (A, (D23, U26, X28A)), UPB: (B, (U22, D27, X28B))}
TERMS = (C0, C1, C2)
SHIFT = (SHIFT_A, SHIFT_B)
WAITS = {
    U0A: (U0A,), U0B: (U0B,), D0A: (D0A,), D0B: (D0B,), X0A: (X0A,), X0B: (X0B,),
    F7: (F7,), F8: (F8,), R12: (GA, GB), R13: (U4A, U4B, BU), R14: (D5A, D5B, BD),
    KEYS: (S0, S9, S10, S6, S15, S12, S13, S14), CHIP: TERMS,
    RFA: (H19A,), RFB: (H19B,), RCA: (D21A, U20A), RCB: (U20B, D21B),
    RLU: (U24, PA), RLD: (D25, PB), UPA: FINAL[UPA][1], UPB: FINAL[UPB][1],
    SHIFT_A: (SHIFT_A,), SHIFT_B: (SHIFT_B,),
}
GROUP = {name: list(WAITS).index(group) for group, names in WAITS.items() for name in names}
SIZE = (3, 1, 2)
PLACE, LANDED = {}, 0
for step in (RFA, RFB, RCA, RCB, RLU, RLD, UPA, UPB):
    for name in WAITS[step]:
        PLACE[name] = (LANDED, SIZE[REDUCE[name][3]])
        LANDED += SIZE[REDUCE[name][3]]
SENT = (
    sum(SIZE[which] * (1, 1, 2)[rows_of] for _, _, rows_of, which, _, _ in GATHER.values())
    + sum(size for _, size in PLACE.values()) + 96
)


def kernel(
    heads, groups,
    q_hbm, k_hbm, v_hbm, rate_hbm, state_hbm, init_hbm, gain_hbm,
    out_ref, state_out_ref,
    q, k, v, rate, init, gain, cur, w, grad, acc, moved, land_c, land,
    in_sem, send_sem, recv_sem, shift_sem, go_sem,
):
    g = lax.axis_index("group")
    me = lax.axis_index("shard")
    x, y, c = me // 8, (me // 2) % 4, me % 2
    xo, co = 1 - x, 1 - c
    yp, ym, yo = (y + 1) % 4, (y + 3) % 4, (y + 2) % 4
    up, down = (g, x * 8 + yp * 2 + c), (g, x * 8 + ym * 2 + c)
    pair, sib = (g, xo * 8 + y * 2 + c), (g, x * 8 + y * 2 + co)
    middle = groups // 2 - 1
    across = xo * 8 + y * 2 + c
    ahead = ((g + 1) % groups, jnp.where(g == middle, across, me))
    behind = ((g + groups - 1) % groups, me)
    jobs = 2 * heads
    rows = w.shape[5]
    half = rows // 2
    part = (pl.ds(0, half), pl.ds(half, half), pl.ds(0, rows))
    mats = (pl.ds(0, 3), pl.ds(0, 1), pl.ds(1, 2))
    column, ring = (x, xo), (y, yp, yo, ym)
    swapped = g == middle + 1
    xs = jnp.where(swapped, xo, x)
    gather_column = ((x, xo),) * heads + ((xs, 1 - xs),) * heads
    to = (up, down, pair, sib)
    origin = ((0, 3), (0, 1), (1, 0), (0, 0))

    def copy(name, j):
        sem = send_sem.at[j]
        if name in GATHER:
            px, py, rows_of, which, way, needs = GATHER[name]
            src = w.at[j, mats[which], gather_column[j][px], ring[py], c, part[rows_of], :]
            dst, target = src, to[way]
        elif name in TERMS:
            m = TERMS.index(name)
            src, dst, target = grad.at[j, m, :, :, co], land_c.at[j, m], sib
        elif name in REDUCE:
            px, py, rows_of, which, way = REDUCE[name]
            src = acc.at[j, mats[which], column[px], ring[py], part[rows_of], :]
            dst, target = land.at[j, pl.ds(*PLACE[name])], to[way]
        else:
            n = SHIFT.index(name)
            src, dst = moved.at[j, :, part[n], :], w.at[j + heads, :, x, y, c, part[n], :]
            target, sem = ahead, shift_sem.at[j, n]
        return pltpu.make_async_remote_copy(
            src_ref=src, dst_ref=dst, send_sem=sem, recv_sem=recv_sem.at[j, GROUP[name]],
            device_id=target, device_id_type=MESH,
        )

    def arrived(j, group):
        names = WAITS[group]
        if group == KEYS:
            place = w.at[j, :, :, :, co]
        elif group == CHIP:
            place = land_c.at[j]
        elif group in SHIFT:
            place = w.at[j + heads, :, xs, y, c, part[SHIFT.index(group)], :]
        elif names[0] in GATHER:
            px, py, rows_of, which, way, needs = GATHER[names[0]]
            px, py = (px + origin[way][0]) % 2, (py + origin[way][1]) % 4
            place = w.at[j, :, gather_column[j][px], ring[py], c, part[rows_of if len(names) == 1 else AB], :]
        else:
            place = land.at[j, pl.ds(PLACE[names[0]][0], sum(PLACE[name][1] for name in names))]
        pltpu.make_async_remote_copy(
            src_ref=place, dst_ref=place, send_sem=send_sem.at[j], recv_sem=recv_sem.at[j, list(WAITS).index(group)],
            device_id=sib, device_id_type=MESH,
        ).wait_recv()

    here = set()

    def need(j, *groups_of):
        for group in groups_of:
            if (group, j) not in here:
                here.add((group, j))
                arrived(j, group)

    def compute(j):
        need(j, KEYS)
        tokens, depth = q.shape[1], q.shape[2]
        slot, head = divmod(j, heads)

        def weight(m):
            return w[j, m].reshape(depth, w.shape[6])

        rows_in = k[j]
        gate = jnp.dot(rows_in, weight(0), preferred_element_type=f32)
        value = jnp.dot(rows_in, weight(1), preferred_element_type=f32)
        sig = jax.nn.sigmoid(gate)
        hidden = (gate * sig * value).astype(bf16)
        guess = lax.dot_general(hidden, weight(2), (((1,), (1,)), ((), ())), preferred_element_type=f32)
        scale = jnp.broadcast_to(rate[head, pl.ds(slot, 1)], (depth, tokens)).T
        error = (scale * (guess - v[j].astype(f32))).astype(bf16)
        back = jnp.dot(error, weight(2), preferred_element_type=f32)
        d_gate = (back * value * sig * (1.0 + gate * (1.0 - sig))).astype(bf16)
        d_up = (back * gate * sig).astype(bf16)
        key_t, err_t = rows_in.T, error.T
        for m, (left, right) in enumerate(((key_t, d_gate), (key_t, d_up), (err_t, hidden))):
            term = jnp.dot(left, right, preferred_element_type=f32)
            grad[j, m] = term.reshape(grad.shape[2:])
            copy(TERMS[m], j).start()

    def queries(j):
        depth, head = q.shape[2], j % heads

        def weight(m):
            return w[j, m].reshape(depth, w.shape[6])

        gate = jnp.dot(q[j], weight(0), preferred_element_type=f32)
        value = jnp.dot(q[j], weight(1), preferred_element_type=f32)
        hidden = (gate * jax.nn.sigmoid(gate) * value).astype(bf16)
        applied = lax.dot_general(hidden, weight(2), (((1,), (1,)), ((), ())), preferred_element_type=f32)
        mean = jnp.mean(applied * applied, axis=-1, keepdims=True)
        normed = applied * lax.rsqrt(mean + epsilon) * gain[pl.ds(head, 1)]
        out_ref[j] = normed.astype(bf16)

    def chip(j):
        need(j, CHIP)
        for m in range(3):
            acc[j, m] = (grad[j, m, :, :, c] + land_c[j, m]).astype(bf16)

    def landed(j, name, which):
        first, size = PLACE[name]
        skip = 1 if which == REST and size == 3 else 0
        return land[j, pl.ds(first + skip, SIZE[which])].astype(f32)

    def add(j, name):
        px, py, rows_of, terms = ADD[name]
        need(j, name)
        sum_at = (column[px], ring[py], part[rows_of])
        split = terms[1][1] if len(terms) == 2 else None
        for which in (GATE, REST) if split else (ALL,):
            at = (j, mats[which], column[px], ring[py])
            mine = grad[at + (c, part[rows_of])] + land_c[at + (part[rows_of],)]
            total = mine + landed(j, terms[0][0], which)
            if which == split:
                total = total + landed(j, terms[1][0], which)
            acc[(j, mats[which]) + sum_at] = total.astype(bf16)

    def final(j, name):
        rows_of, terms = FINAL[name]
        need(j, name)
        total = grad[j, :, x, y, c, part[rows_of]] + land_c[j, :, x, y, part[rows_of]]
        for term in terms:
            total = total + landed(j, term, ALL)
        if j < heads:
            old = cur[j, :, part[rows_of]]
        else:
            came = w[j, :, x, y, c, part[rows_of]].astype(f32)
            old = jnp.where(g == 0, init[j - heads, :, part[rows_of]], came)
        new = old - total * (1.0 / float(q.shape[1] * 16))
        if j < heads:
            moved[j, :, part[rows_of]] = new.astype(bf16)
        else:
            state_out_ref[j - heads, :, part[rows_of]] = new

    def take(j, name):
        @pl.when(g > 0)
        def _():
            arrived(j - heads, name)

    passed_on = set()

    def pass_on(j, name):
        first = not passed_on
        passed_on.add(name)

        @pl.when(g < groups - 1)
        def _():
            if first:
                @pl.when(g == middle)
                def _():
                    pl.semaphore_wait(go_sem, 1)
            copy(name, j).start()

    started = set()

    def take_step(name, j):
        if name == KEYS:
            if not started:
                started.add(name)
                for one in loads[1:]:
                    one.wait()

                @pl.when(g == 0)
                def _():
                    for h in range(heads):
                        w[heads + h, :, x, y, c] = init[h].astype(bf16)

            compute(j)
        elif name == QUERIES:
            queries(j)
        elif name == CHIP:
            chip(j)
        elif name in ADD:
            add(j, name)
        elif name in FINAL:
            final(j, name)
        elif name in (ISA, ISB):
            take(j, SHIFT[name - ISA])
        elif name in SHIFT:
            pass_on(j, name)
        else:
            if name in GATHER:
                need(j, *GATHER[name][5])
            copy(name, j).start()

    def load(n, src, dst):
        return pltpu.make_async_copy(src, dst, in_sem.at[n])

    loads = [
        load(0, state_hbm, cur), load(1, q_hbm, q), load(2, k_hbm, k), load(3, v_hbm, v),
        load(4, rate_hbm, rate), load(5, init_hbm, init), load(6, gain_hbm, gain),
    ]
    for one in loads:
        one.start()
    barrier = pltpu.get_barrier_semaphore()

    def hello(other):
        pl.semaphore_signal(barrier, inc=1, device_id=other, device_id_type=MESH)

    for other in (up, down, pair, sib):
        hello(other)

    @pl.when((g > 0) & (g != middle + 1))
    def _():
        hello(behind)

    @pl.when((g == middle) | (g == middle + 1))
    def _():
        hello((groups - 1, jnp.where(g == middle, across, me)))

    loads[0].wait()
    for h in range(heads):
        w[h, :, x, y, c] = cur[h].astype(bf16)
    near = jnp.where(g == middle, 4, jnp.where(g == groups - 1, 6, 5))
    pl.semaphore_wait(barrier, near)

    @pl.when(g == groups - 1)
    def _():
        pl.semaphore_signal(go_sem, inc=1, device_id=(middle, across), device_id_type=MESH)

    for step in SCHEDULE:
        take_step(step // 6, step % 6)

    for j in range(jobs):
        blocks = land.at[:, pl.ds(0, SENT // jobs)]
        pltpu.make_async_remote_copy(
            src_ref=blocks, dst_ref=blocks, send_sem=send_sem.at[j], recv_sem=recv_sem.at[j, 0],
            device_id=sib, device_id_type=MESH,
        ).wait_send()

    @pl.when(g < groups - 1)
    def _():
        for h in range(heads):
            for name in SHIFT:
                copy(name, h).wait_send()


def on_device(queries, key_tokens, value_tokens, token_rate, state_in, init_state, norm_gain):
    slots, heads, tokens, depth = queries.shape
    rows, hidden = init_state.shape[1], init_state.shape[3]
    jobs = slots * heads
    groups = lax.axis_size("group")
    half = rows // 2
    state = jnp.transpose(state_in[0], (0, 2, 1, 3))
    init = jnp.transpose(init_state, (0, 2, 1, 3))
    any_spec, vmem = pl.BlockSpec(memory_space=pl.ANY), pl.BlockSpec(memory_space=pltpu.VMEM)
    V = pltpu.VMEM
    out, new = pl.pallas_call(
        functools.partial(kernel, heads, groups),
        out_shape=(
            pltpu.VMEM((jobs, tokens, depth), bf16),
            pltpu.VMEM((heads, 3, rows, hidden), f32),
        ),
        in_specs=[any_spec] * 7,
        out_specs=(vmem, vmem),
        scratch_shapes=[
            V((jobs, tokens, depth), bf16), V((jobs, tokens, depth), bf16), V((jobs, tokens, depth), bf16),
            V((heads, slots, tokens), f32), V((heads, 3, rows, hidden), f32), V((heads, depth), f32),
            V((heads, 3, rows, hidden), f32),
            V((jobs, 3, 2, 4, 2, rows, hidden), bf16), V((jobs, 3, 2, 4, 2, rows, hidden), f32),
            V((jobs, 3, 2, 4, rows, hidden), bf16), V((heads, 3, rows, hidden), bf16),
            V((jobs, 3, 2, 4, rows, hidden), f32), V((jobs, LANDED, half, hidden), bf16),
            pltpu.SemaphoreType.DMA((7,)), pltpu.SemaphoreType.DMA((jobs,)),
            pltpu.SemaphoreType.DMA((jobs, len(WAITS))), pltpu.SemaphoreType.DMA((heads, 2)),
            pltpu.SemaphoreType.REGULAR,
        ],
        compiler_params=pltpu.CompilerParams(
            collective_id=0, has_side_effects=True, vmem_limit_bytes=60 * 1024 * 1024
        ),
    )(
        queries.reshape(jobs, tokens, depth), key_tokens.reshape(jobs, tokens, depth),
        value_tokens.reshape(jobs, tokens, depth), jnp.transpose(token_rate, (1, 0, 2)), state, init,
        norm_gain,
    )
    return out.reshape(queries.shape), jnp.transpose(new, (0, 2, 1, 3))[None]


def solution(mesh):
    in_specs = (
        P(None, None, ("group", "shard"), None),
        P(None, None, ("group", "shard"), None),
        P(None, None, ("group", "shard"), None),
        P(None, None, ("group", "shard")),
        P("group", None, "shard", None, None),
        P(None, "shard", None, None),
        P(),
    )
    out_specs = (P(None, None, ("group", "shard"), None), P("group", None, "shard", None, None))
    return jax.shard_map(
        on_device, mesh=mesh, in_specs=in_specs, out_specs=out_specs, check_vma=False
    )
```
